512 devices in a mesh: tm: 16 (over y, core), vert: 32 (over x, z).
Axes of the slice: x: 4, y: 8, z: 8, core: 2. Of those that a mesh axis runs over, the one named last changes fastest.
Arguments:
- features: bfloat16 [16, 16384, 1024], P('tm', 'vert'), may hold values from -6 to 6
- graph_weight: bfloat16 [1024, 1024], P('vert'), may hold values from -0.1875 to 0.1875
- head_weight: bfloat16 [16, 192, 1024], P('tm'), may hold values from -16 to 16
- send_rows: int32 [16, 32, 32, 16], P('tm', 'vert'), may hold values from 0 to 511, as said below
- send_count: int32 [16, 32, 32], P('tm', 'vert'), may hold values from 0 to 16, as said below
- block_index: int32 [16, 128, 3], P('tm', 'vert'), may hold values from 0 to 7, as said below
- block_values: bfloat16 [16, 16384, 3, 128], P('tm', 'vert'), may hold values from -0.3125 to 0.3125
Outputs:
- combined: bfloat16 [16, 16384, 1024], P('tm', 'vert')
The draws below stay inside these ranges and needn't reach their ends.
Inputs may be any that keep to these rules, and one draw needn't show every extreme that they name: send_rows[s, p, q] holds 16 distinct local rows of partition p; slots from send_count[s, p, q] on are ignored. send_count[s, p, p] is 0; in every snapshot some pairs reach 16. `block_index`: the 3 entries of a block row are distinct; column blocks below 4 are the partition's own rows, the others its boundary rows in the order of columns.
All inputs are finite; a program needn't handle non-finite values.
Results may differ from the reference program's by a relative error of at most 0.0075.
Values may be sent and summed in bfloat16 or wider, within the bound.
A program may use at most 64 MiB of HBM per device.

```python
import jax
import jax.numpy as jnp
from jax import lax

D = 1024
HEADS = 16
HS = 64
BLK = 128
NBLK = 3
BMAX = 16
V_DEV = 512
SNAPS = 16
NPART = 32
VERTS = 16384
LB = 4
CB = 8


def draw_head_weight(key, part):
    scale = D ** (-0.5)
    base = jax.random.normal(jax.random.fold_in(key, 11), (HEADS, 3 * HS, D), jnp.float32) * scale
    base = jnp.clip(base, -6.0 * scale, 6.0 * scale)
    return base.astype(jnp.bfloat16)


def draw_send_rows(key, part):
    keys_all = jax.random.split(jax.random.fold_in(key, 21), SNAPS * NPART * NPART)
    rows_all = jax.vmap(lambda single: jax.random.permutation(single, V_DEV)[:BMAX])(keys_all)
    return rows_all.reshape(SNAPS, NPART, NPART, BMAX).astype(jnp.int32)


def draw_send_count(key, part):
    level = jax.random.randint(jax.random.fold_in(key, 31), (SNAPS, 1, NPART), 1, 5)
    base = jax.random.randint(jax.random.fold_in(key, 32), (SNAPS, NPART, NPART), 0, (BMAX + 3) // 4 + 1)
    counts = jnp.minimum(base * level, BMAX)
    source = jnp.arange(NPART)[:, None]
    target = jnp.arange(NPART)[None, :]
    counts = jnp.where((target == (source + 1) % NPART)[None], BMAX, counts)
    counts = jnp.where((target == source)[None], 0, counts)
    return counts.astype(jnp.int32)


def draw_block_index(key, part):
    keys_all = jax.random.split(jax.random.fold_in(key, 41), SNAPS * NPART * LB)
    picks = jax.vmap(lambda single: jax.random.permutation(single, CB)[:NBLK])(keys_all)
    return picks.reshape(SNAPS, NPART * LB, NBLK).astype(jnp.int32)


def block_levels(rng, shape, cuts, low, largest):
    def one(dim, blocks):
        steps = jax.random.uniform(jax.random.fold_in(jax.random.fold_in(rng, 6), dim), (blocks,), jnp.float32, low / len(cuts), largest / len(cuts))
        return jnp.repeat(jnp.exp(steps), shape[dim] // blocks).reshape((-1,) + (1,) * (len(shape) - dim - 1))

    loudness = one(*cuts[0])
    for cut in cuts[1:]:
        loudness = loudness * one(*cut)
    return loudness


def gaussian(rng, extent, deviation, limit, pieces=(), kind=jnp.bfloat16):
    drawn = jax.random.normal(rng, extent, jnp.float32) * deviation
    if len(pieces) > 0:
        drawn = block_levels(rng, extent, pieces, -0.22, 0.18) * drawn
    return jnp.clip(drawn, min=-limit, max=limit).astype(kind)


def setup_inputs(seed: int = 0) -> dict:
    key_list = jax.random.split(jax.random.key(seed), 8)
    return {
        "features": gaussian(key_list[0], (SNAPS, VERTS, D), 1.0, 6.0, ((0, 16), (1, 32))),
        "graph_weight": gaussian(key_list[1], (D, D), D ** -0.5, 0.1875, ((0, 32),)),
        "head_weight": draw_head_weight(jax.random.fold_in(key_list[7], 71), 0),
        "send_rows": draw_send_rows(jax.random.fold_in(key_list[7], 71), 0),
        "send_count": draw_send_count(jax.random.fold_in(key_list[7], 71), 0),
        "block_index": draw_block_index(jax.random.fold_in(key_list[7], 71), 0),
        "block_values": gaussian(key_list[6], (SNAPS, VERTS, NBLK, BLK), (NBLK * BLK) ** -0.5, 0.3125, ((0, 16), (1, 32))),
    }


def graph_snapshot(features_s, graph_weight, rows_s, count_s, index_s, values_s):
    projected = jnp.dot(features_s, graph_weight, preferred_element_type=jnp.float32).astype(jnp.bfloat16)
    projected_parts = projected.reshape(NPART, V_DEV, D)
    slot_ids = jnp.arange(BMAX, dtype=jnp.int32)

    def partition_step(part_id):
        rows_q = rows_s[:, part_id, :]
        count_q = count_s[:, part_id]
        picked = jax.vmap(lambda part_rows, row_ids: part_rows[row_ids])(projected_parts, rows_q)
        live_slots = slot_ids[None, :] < count_q[:, None]
        picked = jnp.where(live_slots[:, :, None], picked, jnp.zeros_like(picked))
        own_rows = lax.dynamic_index_in_dim(projected_parts, part_id, 0, keepdims=False)
        columns = jnp.concatenate([own_rows, picked.reshape(NPART * BMAX, D)], axis=0).reshape(CB, BLK, D)
        index_q = lax.dynamic_slice_in_dim(index_s, (part_id * LB).astype(jnp.int32), LB, 0)
        values_q = lax.dynamic_slice_in_dim(values_s, (part_id * V_DEV).astype(jnp.int32), V_DEV, 0)
        values_q = values_q.reshape(LB, BLK, NBLK, BLK)
        chosen = columns[index_q]
        summed = jnp.einsum("rikj,rkjd->rid", values_q.astype(jnp.float32), chosen.astype(jnp.float32))
        pre_act = own_rows.astype(jnp.float32) + summed.reshape(V_DEV, D)
        return jax.nn.relu(pre_act).astype(jnp.bfloat16)

    return lax.map(partition_step, jnp.arange(NPART, dtype=jnp.int32))


def attend_block(hidden_block, head_weight):
    packed = jnp.einsum("tvd,hcd->tvhc", hidden_block.astype(jnp.float32), head_weight.astype(jnp.float32))
    queries = packed[..., :HS].astype(jnp.bfloat16).astype(jnp.float32)
    keys_part = packed[..., HS:2 * HS].astype(jnp.bfloat16).astype(jnp.float32)
    values = packed[..., 2 * HS:].astype(jnp.bfloat16).astype(jnp.float32)
    scores = jnp.einsum("tvhc,svhc->vhts", queries, keys_part) * (HS ** -0.5)
    causal = jnp.arange(SNAPS)[:, None] >= jnp.arange(SNAPS)[None, :]
    scores = jnp.where(causal, scores, -1e30)
    row_max = jnp.max(scores, axis=-1, keepdims=True)
    exponent = jnp.where(causal, jnp.exp(scores - row_max), 0.0)
    attention = (exponent / jnp.sum(exponent, axis=-1, keepdims=True)).astype(jnp.bfloat16).astype(jnp.float32)
    attended = jnp.einsum("vhts,svhc->tvhc", attention, values)
    return attended.astype(jnp.bfloat16).reshape(SNAPS, V_DEV, D)


def reference(features, graph_weight, head_weight, send_rows, send_count, block_index, block_values):
    hidden = lax.map(
        lambda items: graph_snapshot(items[0], graph_weight, items[1], items[2], items[3], items[4]),
        (features, send_rows, send_count, block_index, block_values))
    attended = lax.map(lambda part_id: attend_block(hidden[:, part_id], head_weight),
                       jnp.arange(NPART, dtype=jnp.int32))
    attended = jnp.transpose(attended, (1, 0, 2, 3)).reshape(SNAPS, VERTS, D)
    hidden = hidden.reshape(SNAPS, VERTS, D)
    return (hidden.astype(jnp.float32) + attended.astype(jnp.float32)).astype(jnp.bfloat16)
```

```python
import functools

import jax
import jax.numpy as jnp
from jax import lax
from jax.experimental import pallas as pl
from jax.experimental.pallas import tpu as pltpu
from jax.sharding import PartitionSpec as P

BF16 = jnp.bfloat16
F32 = jnp.float32
VERT = 32
TM = 16
YS = 8
XS = 4
CHUNKS = 4
WIDE = 256


def dot_last(left, right):
    return lax.dot_general(left, right, (((1,), (1,)), ((), ())), preferred_element_type=F32)


def dot_first(left, right):
    return lax.dot_general(left, right, (((0,), (0,)), ((), ())), preferred_element_type=F32)


def layer_kernel(
    feat, weight, heads, rows, edges, out,
    wg, hwg, proj, picked, recv, hid, xg, att, ret, sel, bias,
    w1_s, w1_r, wr_s, wr_r, wl_s, wl_r, wp_s, wp_r,
    hr_s, hr_r, hl_s, hl_r, x1_s, x1_r, x2_s, x2_r, hp_s, hp_r,
    b_s, b_r, g_s, g_r, a_s, a_r,
):
    v = lax.axis_index("vert")
    m = lax.axis_index("tm")
    y = m // 2
    c = m % 2
    x = v // 8
    z = v % 8

    def to_tm(yy, cc):
        return {"tm": lax.rem(yy + YS, YS) * 2 + cc}

    def copy(src, dst, ssem, rsem, dev):
        return pltpu.make_async_remote_copy(
            src_ref=src, dst_ref=dst, send_sem=ssem, recv_sem=rsem,
            device_id=dev, device_id_type=pl.DeviceIdType.MESH,
        )

    def loop(lo, hi, body):
        def step(i, carry):
            body(i)
            return carry
        lax.fori_loop(lo, hi, step, 0)

    barrier = pltpu.get_barrier_semaphore()
    loop(1, VERT, lambda k: pl.semaphore_signal(
        barrier, inc=1, device_id={"vert": lax.rem(v + k, VERT)}, device_id_type=pl.DeviceIdType.MESH))
    loop(1, TM, lambda k: pl.semaphore_signal(
        barrier, inc=1, device_id={"tm": lax.rem(m + k, TM)}, device_id_type=pl.DeviceIdType.MESH))
    pl.semaphore_wait(barrier, VERT + TM - 2)

    tile_cols = pl.ds(pl.multiple_of(y * 128, 128), 128)
    tile_rows = pl.ds(pl.multiple_of(c * 16, 16), 16)

    def w1(k, q):
        return copy(weight.at[tile_rows, tile_cols], wg.at[y, v, c], w1_s.at[k], w1_r.at[k], {"vert": q})

    def w1_in(k):
        q = lax.rem(v - k + VERT, VERT)
        return copy(weight.at[tile_rows, tile_cols], wg.at[y, q, c], w1_s.at[k], w1_r.at[k], {"vert": q})

    loop(1, VERT, lambda k: w1(k, lax.rem(v + k, VERT)).start())
    wg[y, v, c] = weight[tile_rows, tile_cols]
    hwg[y, c, x] = heads[x]
    sel[...] = (rows[...] == lax.broadcasted_iota(jnp.int32, (512, 512), 1)).astype(BF16)
    ri = lax.broadcasted_iota(jnp.int32, (256, 256), 0)
    ci = lax.broadcasted_iota(jnp.int32, (256, 256), 1)
    bias[...] = jnp.where(((ri & 15) == (ci & 15)) & (ri <= ci), 0.0, -1e30)
    loop(1, VERT, lambda k: w1_in(k).wait_recv())

    def pos(d):
        return lax.rem(y + d + 2 * YS, YS)

    def wpart(d, half):
        if half is None:
            return wg.at[pos(d), :, c]
        return wg.at[pos(d), pl.ds(half * 16, 16), c]

    def hpart(d, half):
        if half is None:
            return hwg.at[pos(d), c, x]
        return hwg.at[pos(d), c, x, :, pl.ds(half * 512, 512)]

    def up(part, s_sem, r_sem, s):
        half = 0 if s == 4 else None
        ref = part(1 - s, half)
        return copy(ref, ref, s_sem.at[s], r_sem.at[s], to_tm(y + 1, c))

    def up_in(part, s_sem, r_sem, s):
        half = 0 if s == 4 else None
        ref = part(-s, half)
        return copy(ref, ref, s_sem.at[s], r_sem.at[s], to_tm(y + 1, c))

    def down(part, s_sem, r_sem, s):
        half = 1 if s == 4 else None
        ref = part(s - 1, half)
        return copy(ref, ref, s_sem.at[s], r_sem.at[s], to_tm(y - 1, c))

    def down_in(part, s_sem, r_sem, s):
        half = 1 if s == 4 else None
        ref = part(s, half)
        return copy(ref, ref, s_sem.at[s], r_sem.at[s], to_tm(y - 1, c))

    def wpartner(d):
        ref = wg.at[pos(d), :, c]
        i = d % YS
        return copy(ref, ref, wp_s.at[i], wp_r.at[i], to_tm(y, 1 - c))

    def wpartner_in(d):
        ref = wg.at[pos(d), :, 1 - c]
        i = d % YS
        return copy(ref, ref, wp_s.at[i], wp_r.at[i], to_tm(y, 1 - c))

    for s in range(1, 5):
        up(wpart, wr_s, wr_r, s).start()
        down(wpart, wl_s, wl_r, s).start()
        if s == 1:
            wpartner(0).start()
        up_in(wpart, wr_s, wr_r, s).wait_recv()
        down_in(wpart, wl_s, wl_r, s).wait_recv()
        if s < 4:
            wpartner(-s).start()
            wpartner(s).start()
        else:
            wpartner(4).start()
    up(hpart, hr_s, hr_r, 1).start()
    down(hpart, hl_s, hl_r, 1).start()
    for d in range(YS):
        wpartner_in(d).wait_recv()

    def boundary(ch, k, q):
        return copy(picked.at[ch, q], recv.at[ch, v], b_s.at[ch, k], b_r.at[ch, k], {"vert": q})

    def boundary_in(ch, k):
        q = lax.rem(v - k + VERT, VERT)
        return copy(picked.at[ch, q], recv.at[ch, q], b_s.at[ch, k], b_r.at[ch, k], {"vert": q})

    for ch in range(CHUNKS):
        wide = jnp.concatenate(
            [wg[2 * ch].reshape(1024, 128), wg[2 * ch + 1].reshape(1024, 128)], axis=1)
        part = jnp.dot(feat[...], wide, preferred_element_type=F32).astype(BF16)
        proj[ch] = part
        rows_out = jnp.dot(sel[...], part, preferred_element_type=F32).astype(BF16)
        picked[ch] = rows_out.reshape(VERT, 16, WIDE)
        loop(1, VERT, lambda k: boundary(ch, k, lax.rem(v + k, VERT)).start())
        recv[ch, v] = picked[ch, v]

    for s in range(1, 5):
        up_in(hpart, hr_s, hr_r, s).wait_recv()
        down_in(hpart, hl_s, hl_r, s).wait_recv()
        if s < 4:
            up(hpart, hr_s, hr_r, s + 1).start()
            down(hpart, hl_s, hl_r, s + 1).start()

    xr = lax.rem(x + 1, XS)
    xl = lax.rem(x + 3, XS)
    xo = lax.rem(x + 2, XS)
    right = {"vert": xr * 8 + z}
    left = {"vert": xl * 8 + z}

    def x1(g, side):
        ref = hwg.at[pl.ds(2 * g, 2), c, x]
        return copy(ref, ref, x1_s.at[side, g], x1_r.at[side, g], right if side == 0 else left)

    def x1_in(g, side):
        ref = hwg.at[pl.ds(2 * g, 2), c, xl if side == 0 else xr]
        return copy(ref, ref, x1_s.at[side, g], x1_r.at[side, g], right if side == 0 else left)

    def x2(g, side):
        ref = hwg.at[2 * g + side, c, xl if side == 0 else xr]
        return copy(ref, ref, x2_s.at[side, g], x2_r.at[side, g], right if side == 0 else left)

    def x2_in(g, side):
        ref = hwg.at[2 * g + side, c, xo]
        return copy(ref, ref, x2_s.at[side, g], x2_r.at[side, g], right if side == 0 else left)

    def hpartner(g):
        ref = hwg.at[pl.ds(2 * g, 2), c]
        return copy(ref, ref, hp_s.at[g], hp_r.at[g], to_tm(y, 1 - c))

    def hpartner_in(g):
        ref = hwg.at[pl.ds(2 * g, 2), 1 - c]
        return copy(ref, ref, hp_s.at[g], hp_r.at[g], to_tm(y, 1 - c))

    for g in range(CHUNKS):
        x1(g, 0).start()
        x1(g, 1).start()

    def regroup(ch, k, t):
        return copy(hid.at[ch, t], xg.at[ch, :, m], g_s.at[ch, k], g_r.at[ch, k], {"tm": t})

    def regroup_in(ch, k):
        t = lax.rem(m - k + TM, TM)
        return copy(hid.at[ch, t], xg.at[ch, :, t], g_s.at[ch, k], g_r.at[ch, k], {"tm": t})

    for ch in range(CHUNKS):
        acc = proj[ch].astype(F32) + jnp.dot(edges[:, :512], proj[ch], preferred_element_type=F32)
        loop(1, VERT, lambda k: boundary_in(ch, k).wait_recv())
        acc = acc + jnp.dot(
            edges[:, 512:], recv[ch].reshape(512, WIDE), preferred_element_type=F32)
        hid[ch] = jnp.maximum(acc, 0.0).astype(BF16).reshape(TM, 2, 16, WIDE)
        loop(1, TM, lambda k: regroup(ch, k, lax.rem(m + k, TM)).start())
        xg[ch, :, m] = hid[ch, m]
        for side in range(2):
            x1_in(ch, side).wait_recv()
        for side in range(2):
            x2(ch, side).start()
    for side in range(2):
        x2_in(0, side).wait_recv()
    hpartner(0).start()
    for ch in range(CHUNKS):
        loop(1, TM, lambda k: regroup_in(ch, k).wait_recv())

    def give(g, k, t):
        return copy(att.at[g, :, t], ret.at[g, m], a_s.at[g, k], a_r.at[g, k], {"tm": t})

    def give_in(g, k):
        t = lax.rem(m - k + TM, TM)
        return copy(att.at[g, :, t], ret.at[g, t], a_s.at[g, k], a_r.at[g, k], {"tm": t})

    for g in range(CHUNKS):
        if g + 1 < CHUNKS:
            for side in range(2):
                x2_in(g + 1, side).wait_recv()
            hpartner(g + 1).start()
        hpartner_in(g).wait_recv()
        wide = hwg[pl.ds(2 * g, 2)].reshape(768, 1024)
        packed = dot_last(wide[:, :WIDE], xg[0].reshape(512, WIDE))
        for ch in range(1, CHUNKS):
            packed = packed + dot_last(
                wide[:, ch * WIDE:(ch + 1) * WIDE], xg[ch].reshape(512, WIDE))
        packed = packed.astype(BF16)
        for b in range(2):
            cols = slice(b * 256, (b + 1) * 256)
            outs = []
            for j in range(4):
                query = packed[192 * j:192 * j + 64, cols]
                key = packed[192 * j + 64:192 * j + 128, cols]
                value = packed[192 * j + 128:192 * j + 192, cols]
                score = dot_first(key, query) * 0.125 + bias[...]
                top = jnp.max(score, axis=0, keepdims=True)
                exponent = jnp.exp(score - top)
                scale = 1.0 / jnp.sum(exponent, axis=0, keepdims=True)
                attention = (exponent * scale).astype(BF16)
                outs.append(jnp.dot(value, attention, preferred_element_type=F32))
            block = jnp.concatenate(outs, axis=0)
            att[g, b] = block.T.astype(BF16).reshape(TM, 16, WIDE)
        loop(1, TM, lambda k: give(g, k, lax.rem(m + k, TM)).start())
        ret[g, m] = att[g, :, m]

    for g in range(CHUNKS):
        loop(1, TM, lambda k: give_in(g, k).wait_recv())
        total = hid[g].reshape(512, WIDE).astype(F32) + ret[g].reshape(512, WIDE).astype(F32)
        out[:, g * WIDE:(g + 1) * WIDE] = total.astype(BF16)

    loop(1, VERT, lambda k: w1_in(k).wait_send())
    for s in range(1, 5):
        up(wpart, wr_s, wr_r, s).wait_send()
        down(wpart, wl_s, wl_r, s).wait_send()
        up(hpart, hr_s, hr_r, s).wait_send()
        down(hpart, hl_s, hl_r, s).wait_send()
    for d in range(YS):
        wpartner(d).wait_send()
    for g in range(CHUNKS):
        for side in range(2):
            x1(g, side).wait_send()
            x2(g, side).wait_send()
        hpartner(g).wait_send()
        loop(1, VERT, lambda k: boundary_in(g, k).wait_send())
        loop(1, TM, lambda k: regroup_in(g, k).wait_send())
        loop(1, TM, lambda k: give_in(g, k).wait_send())


def layer(feat, weight, heads, rows, edges):
    dma = pltpu.SemaphoreType.DMA
    vmem = pl.BlockSpec(memory_space=pltpu.VMEM)
    return pl.pallas_call(
        layer_kernel,
        out_shape=jax.ShapeDtypeStruct((512, 1024), BF16),
        in_specs=[vmem] * 5,
        out_specs=vmem,
        scratch_shapes=[
            pltpu.VMEM((YS, VERT, 2, 16, 128), BF16),
            pltpu.VMEM((YS, 2, XS, 48, 1024), BF16),
            pltpu.VMEM((CHUNKS, 512, WIDE), BF16),
            pltpu.VMEM((CHUNKS, VERT, 16, WIDE), BF16),
            pltpu.VMEM((CHUNKS, VERT, 16, WIDE), BF16),
            pltpu.VMEM((CHUNKS, TM, 2, 16, WIDE), BF16),
            pltpu.VMEM((CHUNKS, 2, TM, 16, WIDE), BF16),
            pltpu.VMEM((CHUNKS, 2, TM, 16, WIDE), BF16),
            pltpu.VMEM((CHUNKS, TM, 2, 16, WIDE), BF16),
            pltpu.VMEM((512, 512), BF16),
            pltpu.VMEM((256, 256), F32),
            dma((VERT,)), dma((VERT,)),
            dma((5,)), dma((5,)), dma((5,)), dma((5,)), dma((YS,)), dma((YS,)),
            dma((5,)), dma((5,)), dma((5,)), dma((5,)),
            dma((2, CHUNKS)), dma((2, CHUNKS)), dma((2, CHUNKS)), dma((2, CHUNKS)),
            dma((CHUNKS,)), dma((CHUNKS,)),
            dma((CHUNKS, VERT)), dma((CHUNKS, VERT)),
            dma((CHUNKS, TM)), dma((CHUNKS, TM)),
            dma((CHUNKS, TM)), dma((CHUNKS, TM)),
        ],
        compiler_params=pltpu.CompilerParams(
            collective_id=0, has_side_effects=True, vmem_limit_bytes=56 * 1024 * 1024),
    )(feat, weight, heads, rows, edges)


def shards(features, graph_weight, head_weight, send_rows, send_count, block_index, block_values):
    live = jnp.arange(16)[None, :] < send_count[0, 0][:, None]
    rows = jnp.where(live, send_rows[0, 0], -1).reshape(512, 1)
    edge = block_values[0].reshape(4, 128, 3, 128)
    place = block_index[0][:, None, :, None] == jnp.arange(8)[None, None, None, :]
    zero = jnp.zeros((), BF16)
    edges = sum(
        jnp.where(place[:, :, k, :, None], edge[:, :, k, None, :], zero) for k in range(3)
    ).reshape(512, 1024)
    heads = head_weight[0].reshape(XS, 48, 1024)
    return layer(features[0], graph_weight, heads, rows, edges)[None]


def solution(mesh):
    return jax.shard_map(
        shards,
        mesh=mesh,
        in_specs=(
            P("tm", "vert", None),
            P("vert", None),
            P("tm", None, None),
            P("tm", "vert", None, None),
            P("tm", "vert", None),
            P("tm", "vert", None),
            P("tm", "vert", None, None),
        ),
        out_specs=P("tm", "vert", None),
        check_vma=False,
    )
```

```python
import jax
import jax.numpy as jnp
from jax import lax
from jax.experimental import pallas as pl
from jax.experimental.pallas import tpu as pltpu
from jax.sharding import PartitionSpec as P

BF16 = jnp.bfloat16
F32 = jnp.float32
VERT = 32
TM = 16
YS = 8
XS = 4
WIDE = 256
STEPS = 5
MESH = pl.DeviceIdType.MESH


def dot_last(left, right):
    return lax.dot_general(left, right, (((1,), (1,)), ((), ())), preferred_element_type=F32)


def dot_first(left, right):
    return lax.dot_general(left, right, (((0,), (0,)), ((), ())), preferred_element_type=F32)


def far_first(i, size):
    return lax.rem(size // 2 + (1 - 2 * lax.rem(i, 2)) * ((i + 1) // 2) + size, size)


def layer_kernel(
    feat_in, weight_in, heads, rows_in, count_in, blocks_in, index_in, out,
    feat, weight, rows, count, blocks, index,
    wg, hwg, proj_one, proj_two, picked_one, picked_two, recv_one, recv_two,
    hid, xg, att, ret, sel, edges, bias,
    in_s, w1_s, w1_r, wr_s, wr_r, wl_s, wl_r, wp_s, wp_r,
    hr_s, hr_r, hl_s, hl_r, x1_s, x1_r, x2_s, x2_r, hp_s, hp_r,
    b_s, b_r, g_s, g_r, a_s, a_r,
):
    v = lax.axis_index("vert")
    m = lax.axis_index("tm")
    y = m // 2
    c = lax.rem(m, 2)
    x = v // 8
    z = lax.rem(v, 8)

    def pos(d):
        return lax.rem(y + d + 2 * YS, YS)

    def to_tm(d, cc):
        return {"tm": pos(d) * 2 + cc}

    def copy(src, dst, ssem, rsem, dev):
        return pltpu.make_async_remote_copy(
            src_ref=src, dst_ref=dst, send_sem=ssem, recv_sem=rsem,
            device_id=dev, device_id_type=MESH,
        )

    def loop(lo, hi, body):
        def step(i, carry):
            body(i)
            return carry
        lax.fori_loop(lo, hi, step, 0)

    def vert_peers(body):
        def one(i):
            dx, dz = far_first(i // 8, XS), far_first(lax.rem(i, 8), 8)
            body(lax.rem(x + dx, XS) * 8 + lax.rem(z + dz, 8))
        loop(0, VERT - 1, one)

    def tm_peers(body):
        def one(i):
            body(pos(far_first(i // 2, YS)) * 2 + lax.rem(c + 1 + lax.rem(i, 2), 2))
        loop(0, TM - 1, one)

    barrier = pltpu.get_barrier_semaphore()
    vert_peers(lambda q: pl.semaphore_signal(barrier, inc=1, device_id={"vert": q}, device_id_type=MESH))
    tm_peers(lambda t: pl.semaphore_signal(barrier, inc=1, device_id={"tm": t}, device_id_type=MESH))

    loads = [
        pltpu.make_async_copy(src, dst, in_s.at[i]) for i, (src, dst) in enumerate((
            (rows_in, rows), (count_in, count), (index_in, index), (blocks_in, blocks),
            (weight_in, weight), (heads.at[x], hwg.at[y, c, x]), (feat_in, feat)))
    ]
    for load in loads:
        load.start()

    tile_cols = pl.ds(pl.multiple_of(y * 128, 128), 128)
    tile_rows = pl.ds(pl.multiple_of(c * 16, 16), 16)

    with jax.named_scope("tables"):
        ri = lax.broadcasted_iota(jnp.int32, (256, 256), 0)
        ci = lax.broadcasted_iota(jnp.int32, (256, 256), 1)
        bias[...] = jnp.where(((ri & 15) == (ci & 15)) & (ri <= ci), 0.0, -1e30)
        for load in loads[:5]:
            load.wait()
        wg[y, v, c] = weight[tile_rows, tile_cols]
        live = lax.broadcasted_iota(jnp.int32, (16, VERT), 0) < count[...]
        slots = jnp.where(live, rows[...], 1023)
        lane = lax.broadcasted_iota(jnp.int32, (VERT, 512), 1)
        spread = (lane // 16 == lax.broadcasted_iota(jnp.int32, (VERT, 512), 0)).astype(BF16)
        high = jnp.dot((slots >> 4).astype(F32).astype(BF16), spread, preferred_element_type=F32)
        low = jnp.dot((slots & 15).astype(F32).astype(BF16), spread, preferred_element_type=F32)
        slot = lax.broadcasted_iota(jnp.int32, (16, 512), 0)
        mine = slot == (lax.broadcasted_iota(jnp.int32, (16, 512), 1) & 15)
        wanted = jnp.sum(jnp.where(mine, high * 16.0 + low, 0.0), axis=0, keepdims=True)
        vertex = lax.broadcasted_iota(jnp.int32, (512, 512), 0).astype(F32)
        sel[...] = jnp.where(vertex == wanted, 1.0, 0.0).T.astype(BF16)
        for r in range(4):
            band = slice(r * 128, (r + 1) * 128)
            pieces = [blocks[k, band] for k in range(3)]
            zero = jnp.zeros((128, 128), BF16)
            for b in range(8):
                block = zero
                for k in range(3):
                    block = jnp.where(index[k, 0, r] == b, pieces[k], block)
                edges[band, b * 128:(b + 1) * 128] = block
        loads[5].wait()
    with jax.named_scope("entry"):
        pl.semaphore_wait(barrier, VERT + TM - 2)

    def w1(q):
        return copy(weight.at[tile_rows, tile_cols], wg.at[y, v, c], w1_s.at[0], w1_r.at[0], {"vert": q})

    def w1_all():
        ref = wg.at[y, pl.ds(0, VERT - 1), c]
        return copy(ref, ref, w1_s.at[0], w1_r.at[0], {"vert": lax.rem(v + 1, VERT)})

    def wpart(d, half):
        if half is None:
            return wg.at[pos(d), :, c]
        return wg.at[pos(d), pl.ds(half * 16, 16), c]

    def hpart(d, half):
        if half is None:
            return hwg.at[pos(d), c, x]
        return hwg.at[pos(d), c, x, :, pl.ds(half * 512, 512)]

    def up(part, sems, s):
        ref = part(1 - s, 0 if s == 4 else None)
        return copy(ref, ref, sems[0].at[s], sems[1].at[s], to_tm(1, c))

    def up_in(part, sems, s):
        ref = part(-s, 0 if s == 4 else None)
        return copy(ref, ref, sems[0].at[s], sems[1].at[s], to_tm(1, c))

    def down(part, sems, s):
        ref = part(s - 1, 1 if s == 4 else None)
        return copy(ref, ref, sems[0].at[s], sems[1].at[s], to_tm(-1, c))

    def down_in(part, sems, s):
        ref = part(s, 1 if s == 4 else None)
        return copy(ref, ref, sems[0].at[s], sems[1].at[s], to_tm(-1, c))

    wup, wdown = (wr_s, wr_r), (wl_s, wl_r)
    hup, hdown = (hr_s, hr_r), (hl_s, hl_r)

    def ring_send(part, sems_up, sems_down, s):
        up(part, sems_up, s).start()
        down(part, sems_down, s).start()

    def ring_wait(part, sems_up, sems_down, s):
        up_in(part, sems_up, s).wait_recv()
        down_in(part, sems_down, s).wait_recv()

    def wpartner(d):
        ref = wg.at[pos(d), :, c]
        i = d % YS
        return copy(ref, ref, wp_s.at[i], wp_r.at[i], to_tm(0, 1 - c))

    def wpartner_in(d):
        ref = wg.at[pos(d), :, 1 - c]
        i = d % YS
        return copy(ref, ref, wp_s.at[i], wp_r.at[i], to_tm(0, 1 - c))

    def tiles(s):
        return (0,) if s == 0 else (4,) if s == 4 else (-s, s)

    def store(s, one, two):
        if s == 0:
            return one.at[0]
        if s == 4:
            return one.at[1]
        return two.at[s - 1]

    def width(s):
        return 128 * len(tiles(s))

    def boundary(s, q):
        return copy(store(s, picked_one, picked_two).at[q], store(s, recv_one, recv_two).at[v],
                    b_s.at[s], b_r.at[s], {"vert": q})

    def boundary_all(s):
        most = pl.ds(0, VERT - 1)
        return copy(store(s, picked_one, picked_two).at[most], store(s, recv_one, recv_two).at[most],
                    b_s.at[s], b_r.at[s], {"vert": lax.rem(v + 1, VERT)})

    def project(s):
        with jax.named_scope(f"project{s}"):
            parts = [wg[pos(d)].reshape(1024, 128) for d in tiles(s)]
            wide = parts[0] if len(parts) == 1 else jnp.concatenate(parts, axis=1)
            part = jnp.dot(feat[...], wide, preferred_element_type=F32).astype(BF16)
            store(s, proj_one, proj_two)[...] = part
            rows_out = jnp.dot(sel[...], part, preferred_element_type=F32).astype(BF16)
            picked = store(s, picked_one, picked_two)
            picked[...] = rows_out.reshape(VERT, 16, width(s))
            vert_peers(lambda q: boundary(s, q).start())
            store(s, recv_one, recv_two)[v] = picked[v]

    def regroup(ct, t):
        return copy(hid.at[ct, t], xg.at[ct, :, m], g_s.at[0], g_r.at[0], {"tm": t})

    def regroup_all():
        return copy(hid.at[:, pl.ds(0, TM - 1)], hid.at[:, pl.ds(0, TM - 1)],
                    g_s.at[0], g_r.at[0], to_tm(1, c))

    def convolve(s):
        with jax.named_scope(f"bwait{s}"):
            boundary_all(s).wait_recv()
        with jax.named_scope(f"convolve{s}"):
            part = store(s, proj_one, proj_two)[...]
            acc = part.astype(F32) + jnp.dot(edges[:, :512], part, preferred_element_type=F32)
            acc = acc + jnp.dot(
                edges[:, 512:], store(s, recv_one, recv_two)[...].reshape(512, width(s)),
                preferred_element_type=F32)
            done = jnp.maximum(acc, 0.0).astype(BF16)
            for i, d in enumerate(tiles(s)):
                hid[pos(d)] = done[:, i * 128:(i + 1) * 128].reshape(TM, 2, 16, 128)
            for d in tiles(s):
                tm_peers(lambda t: regroup(pos(d), t).start())
                xg[pos(d), :, m] = hid[pos(d), m]

    xr = lax.rem(x + 1, XS)
    xl = lax.rem(x + 3, XS)
    xo = lax.rem(x + 2, XS)
    sides = ({"vert": xr * 8 + z}, {"vert": xl * 8 + z})

    def x1(d, side):
        ref = hwg.at[pos(d), c, x]
        return copy(ref, ref, x1_s.at[side, d % YS], x1_r.at[side, d % YS], sides[side])

    def x1_in(d, side):
        ref = hwg.at[pos(d), c, (xl, xr)[side]]
        return copy(ref, ref, x1_s.at[side, d % YS], x1_r.at[side, d % YS], sides[side])

    def x2(d, side):
        ref = hwg.at[pos(d), c, (xl, xr)[side], :, pl.ds(512 * side, 512)]
        return copy(ref, ref, x2_s.at[side, d % YS], x2_r.at[side, d % YS], sides[side])

    def x2_in(d, side):
        ref = hwg.at[pos(d), c, xo, :, pl.ds(512 * side, 512)]
        return copy(ref, ref, x2_s.at[side, d % YS], x2_r.at[side, d % YS], sides[side])

    def hpartner(d):
        ref = hwg.at[pos(d), c]
        return copy(ref, ref, hp_s.at[d % YS], hp_r.at[d % YS], to_tm(0, 1 - c))

    def hpartner_in(d):
        ref = hwg.at[pos(d), 1 - c]
        return copy(ref, ref, hp_s.at[d % YS], hp_r.at[d % YS], to_tm(0, 1 - c))

    def x1_send(s):
        for d in tiles(s):
            for side in range(2):
                x1(d, side).start()

    def x2_send(s):
        with jax.named_scope(f"xwait{s}"):
            for d in tiles(s):
                for side in range(2):
                    x1_in(d, side).wait_recv()
                for side in range(2):
                    x2(d, side).start()

    def xdone(s):
        with jax.named_scope(f"xdone{s}"):
            for d in tiles(s):
                for side in range(2):
                    x2_in(d, side).wait_recv()
                hpartner(d).start()

    def wstep(s):
        with jax.named_scope(f"wstep{s}"):
            ring_wait(wpart, wup, wdown, s)
            if s < 4:
                ring_send(wpart, wup, wdown, s + 1)
            for d in tiles(s):
                wpartner(d).start()

    def hstep(s):
        with jax.named_scope(f"hstep{s}"):
            ring_wait(hpart, hup, hdown, s)
            if s < 4:
                ring_send(hpart, hup, hdown, s + 1)
        x1_send(s)

    def wready(s):
        with jax.named_scope(f"wready{s}"):
            for d in tiles(s):
                wpartner_in(d).wait_recv()

    vert_peers(lambda q: w1(q).start())
    ring_send(hpart, hup, hdown, 1)
    x1_send(0)
    hstep(1)
    with jax.named_scope("wtiles"):
        w1_all().wait_recv()
    ring_send(wpart, wup, wdown, 1)
    wpartner(0).start()
    loads[6].wait()
    wready(0)
    project(0)
    hstep(2)
    x2_send(0)
    x2_send(1)
    wstep(1)
    wready(1)
    project(1)
    hstep(3)
    convolve(0)
    wstep(2)
    x2_send(2)
    wready(2)
    project(2)
    hstep(4)
    wstep(3)
    wready(3)
    project(3)
    x2_send(3)
    convolve(1)
    xdone(0)
    xdone(1)
    wstep(4)
    wready(4)
    project(4)
    x2_send(4)
    convolve(2)
    xdone(2)
    convolve(3)
    xdone(3)
    convolve(4)
    xdone(4)
    with jax.named_scope("hready"):
        for d in range(YS):
            hpartner_in(d).wait_recv()
    with jax.named_scope("gwait"):
        regroup_all().wait_recv()

    def give(g, t):
        return copy(att.at[g, :, t], ret.at[g, m], a_s.at[0], a_r.at[g], {"tm": t})

    def give_all(g):
        most = pl.ds(0, TM - 1)
        return copy(ret.at[g, most], ret.at[g, most], a_s.at[0], a_r.at[g], to_tm(1, c))

    def give_out():
        most = pl.ds(0, TM - 1)
        return copy(ret.at[:, most], ret.at[:, most], a_s.at[0], a_r.at[0], to_tm(1, c))

    def attend(g):
        with jax.named_scope("attend"):
            wide = hwg[g].reshape(384, 1024)
            packed = None
            for ch in range(4):
                seen = jnp.concatenate(
                    [xg[2 * ch].reshape(512, 128), xg[2 * ch + 1].reshape(512, 128)], axis=1)
                term = dot_last(wide[:, ch * WIDE:(ch + 1) * WIDE], seen)
                packed = term if packed is None else packed + term
            packed = packed.astype(BF16)
            for b in range(2):
                cols = slice(b * 256, (b + 1) * 256)
                outs = []
                for j in range(2):
                    query = packed[192 * j:192 * j + 64, cols]
                    key = packed[192 * j + 64:192 * j + 128, cols]
                    value = packed[192 * j + 128:192 * j + 192, cols]
                    score = dot_first(key, query) * 0.125 + bias[...]
                    top = jnp.max(score, axis=0, keepdims=True)
                    exponent = jnp.exp(score - top)
                    scale = 1.0 / jnp.sum(exponent, axis=0, keepdims=True)
                    attention = (exponent * scale).astype(BF16)
                    outs.append(jnp.dot(value, attention, preferred_element_type=F32))
                block = jnp.concatenate(outs, axis=0)
                att[g, b] = block.T.astype(BF16).reshape(TM, 16, 128)
            tm_peers(lambda t: give(g, t).start())
            ret[g, m] = att[g, :, m]

    loop(0, YS, attend)

    with jax.named_scope("sent"):
        w1_all().wait_send()
        for s in range(1, 5):
            up(wpart, wup, s).wait_send()
            down(wpart, wdown, s).wait_send()
            up(hpart, hup, s).wait_send()
            down(hpart, hdown, s).wait_send()
        for d in range(YS):
            wpartner(d).wait_send()
            for side in range(2):
                x1(d, side).wait_send()
                x2(d, side).wait_send()
            hpartner(d).wait_send()
        for s in range(STEPS):
            boundary_all(s).wait_send()
        regroup_all().wait_send()

    def finish(g):
        with jax.named_scope("await"):
            give_all(g).wait_recv()
        total = hid[g].reshape(512, 128).astype(F32) + ret[g].reshape(512, 128).astype(F32)
        out[:, pl.ds(pl.multiple_of(g * 128, 128), 128)] = total.astype(BF16)

    loop(0, YS, finish)
    with jax.named_scope("last"):
        give_out().wait_send()


def layer(*operands):
    dma = pltpu.SemaphoreType.DMA
    vmem = pl.BlockSpec(memory_space=pltpu.VMEM)
    hbm = pl.BlockSpec(memory_space=pltpu.HBM)
    return pl.pallas_call(
        layer_kernel,
        out_shape=jax.ShapeDtypeStruct((512, 1024), BF16),
        in_specs=[hbm] * 7,
        out_specs=vmem,
        scratch_shapes=[
            pltpu.VMEM((512, 1024), BF16),
            pltpu.VMEM((32, 1024), BF16),
            pltpu.VMEM((16, VERT), jnp.int32),
            pltpu.VMEM((1, VERT), jnp.int32),
            pltpu.VMEM((3, 512, 128), BF16),
            pltpu.SMEM((3, 1, 4), jnp.int32),
            pltpu.VMEM((YS, VERT, 2, 16, 128), BF16),
            pltpu.VMEM((YS, 2, XS, 48, 1024), BF16),
            pltpu.VMEM((2, 512, 128), BF16),
            pltpu.VMEM((3, 512, WIDE), BF16),
            pltpu.VMEM((2, VERT, 16, 128), BF16),
            pltpu.VMEM((3, VERT, 16, WIDE), BF16),
            pltpu.VMEM((2, VERT, 16, 128), BF16),
            pltpu.VMEM((3, VERT, 16, WIDE), BF16),
            pltpu.VMEM((YS, TM, 2, 16, 128), BF16),
            pltpu.VMEM((YS, 2, TM, 16, 128), BF16),
            pltpu.VMEM((YS, 2, TM, 16, 128), BF16),
            pltpu.VMEM((YS, TM, 2, 16, 128), BF16),
            pltpu.VMEM((512, 512), BF16),
            pltpu.VMEM((512, 1024), BF16),
            pltpu.VMEM((256, 256), F32),
            dma((7,)), dma((1,)), dma((1,)),
            dma((5,)), dma((5,)), dma((5,)), dma((5,)), dma((YS,)), dma((YS,)),
            dma((5,)), dma((5,)), dma((5,)), dma((5,)),
            dma((2, YS)), dma((2, YS)), dma((2, YS)), dma((2, YS)),
            dma((YS,)), dma((YS,)),
            dma((STEPS,)), dma((STEPS,)),
            dma((1,)), dma((1,)),
            dma((1,)), dma((YS,)),
        ],
        compiler_params=pltpu.CompilerParams(
            collective_id=0, has_side_effects=True, vmem_limit_bytes=48 * 1024 * 1024),
    )(*(pltpu.with_memory_space_constraint(op, pltpu.HBM) for op in operands))


def shards(features, graph_weight, head_weight, send_rows, send_count, block_index, block_values):
    heads = head_weight[0].reshape(XS, 48, 1024)
    return layer(
        features[0], graph_weight, heads, send_rows[0, 0].T, send_count[0],
        block_values[0].transpose(1, 0, 2), block_index.transpose(2, 0, 1))[None]


def solution(mesh):
    return jax.shard_map(
        shards,
        mesh=mesh,
        in_specs=(
            P("tm", "vert", None),
            P("vert", None),
            P("tm", None, None),
            P("tm", "vert", None, None),
            P("tm", "vert", None),
            P("tm", "vert", None),
            P("tm", "vert", None, None),
        ),
        out_specs=P("tm", "vert", None),
        check_vma=False,
    )
```

```python
import jax
import jax.numpy as jnp
from jax import lax
from jax.experimental import pallas as pl
from jax.experimental.pallas import tpu as pltpu
from jax.sharding import PartitionSpec as P

BF16 = jnp.bfloat16
F32 = jnp.float32
VERT = 32
TM = 16
YS = 8
XS = 4
WIDE = 256
STEPS = 5
MESH = pl.DeviceIdType.MESH


def dot_last(left, right):
    return lax.dot_general(left, right, (((1,), (1,)), ((), ())), preferred_element_type=F32)


def dot_first(left, right):
    return lax.dot_general(left, right, (((0,), (0,)), ((), ())), preferred_element_type=F32)


def layer_kernel(
    feat_in, weight_in, heads, rows_in, count_in, blocks_in, index_in, out,
    feat, weight, rows, count, blocks, index,
    wg, hwg, proj_one, proj_two, picked_one, picked_two, recv_one, recv_two,
    hid, xg, att, ret, sel, edges, bias,
    in_s, w1_s, w1_r, wr_s, wr_r, wp_s, wp_r,
    hr_s, hr_r, hl_s, hl_r, x1_s, x1_r, x2_s, x2_r, hp_s, hp_r,
    b_s, b_r, g_s, g_r, a_s, a_r,
):
    v = lax.axis_index("vert")
    m = lax.axis_index("tm")
    y = m // 2
    c = lax.rem(m, 2)
    x = v // 8
    z = lax.rem(v, 8)

    def pos(d):
        return lax.rem(y + d + 2 * YS, YS)

    def to_tm(d, cc):
        return {"tm": pos(d) * 2 + cc}

    def copy(src, dst, ssem, rsem, dev):
        return pltpu.make_async_remote_copy(
            src_ref=src, dst_ref=dst, send_sem=ssem, recv_sem=rsem,
            device_id=dev, device_id_type=MESH,
        )

    def loop(lo, hi, body):
        def step(i, carry):
            body(i)
            return carry
        lax.fori_loop(lo, hi, step, 0)

    by_x = [lax.rem(x + dx, XS) * 8 for dx in range(XS)]
    by_z = [lax.rem(z + dz, 8) for dz in range(8)]
    vert_ids = [by_x[dx] + by_z[dz] for dx in (2, 1, 3, 0) for dz in (4, 3, 5, 2, 6, 1, 7, 0)][:-1]
    by_y = [lax.rem(y + dy, YS) * 2 for dy in range(YS)]
    tm_ids = [by_y[dy] + cc for dy in (4, 3, 5, 2, 6, 1, 7, 0) for cc in (1 - c, c)][:-1]

    def vert_peers(body):
        for q in vert_ids:
            body(q)

    def tm_peers(body):
        for t in tm_ids:
            body(t)

    barrier = pltpu.get_barrier_semaphore()
    vert_peers(lambda q: pl.semaphore_signal(barrier, inc=1, device_id={"vert": q}, device_id_type=MESH))
    tm_peers(lambda t: pl.semaphore_signal(barrier, inc=1, device_id={"tm": t}, device_id_type=MESH))

    loads = [
        pltpu.make_async_copy(src, dst, in_s.at[i]) for i, (src, dst) in enumerate((
            (rows_in, rows), (count_in, count), (index_in, index), (blocks_in, blocks),
            (weight_in, weight), (heads.at[x], hwg.at[y, c, x]), (feat_in, feat)))
    ]
    for load in loads:
        load.start()

    tile_cols = [pl.ds(pl.multiple_of(pos(4 * i) * 128, 128), 128) for i in range(2)]
    tile_rows = pl.ds(pl.multiple_of(c * 16, 16), 16)

    with jax.named_scope("tables"):
        ri = lax.broadcasted_iota(jnp.int32, (256, 256), 0)
        ci = lax.broadcasted_iota(jnp.int32, (256, 256), 1)
        bias[...] = jnp.where(((ri & 15) == (ci & 15)) & (ri <= ci), 0.0, -1e30)
        for load in loads[:5]:
            load.wait()
        for i in range(2):
            wg[pos(4 * i), v, c] = weight[tile_rows, tile_cols[i]]
        live = lax.broadcasted_iota(jnp.int32, (16, VERT), 0) < count[...]
        slots = jnp.where(live, rows[...], 1023)
        lane = lax.broadcasted_iota(jnp.int32, (VERT, 512), 1)
        spread = (lane // 16 == lax.broadcasted_iota(jnp.int32, (VERT, 512), 0)).astype(BF16)
        high = jnp.dot((slots >> 4).astype(F32).astype(BF16), spread, preferred_element_type=F32)
        low = jnp.dot((slots & 15).astype(F32).astype(BF16), spread, preferred_element_type=F32)
        slot = lax.broadcasted_iota(jnp.int32, (16, 512), 0)
        mine = slot == (lax.broadcasted_iota(jnp.int32, (16, 512), 1) & 15)
        wanted = jnp.sum(jnp.where(mine, high * 16.0 + low, 0.0), axis=0, keepdims=True)
        vertex = lax.broadcasted_iota(jnp.int32, (512, 512), 0).astype(F32)
        sel[...] = jnp.where(vertex == wanted, 1.0, 0.0).T.astype(BF16)
        for r in range(4):
            band = slice(r * 128, (r + 1) * 128)
            pieces = [blocks[k, band] for k in range(3)]
            zero = jnp.zeros((128, 128), BF16)
            for b in range(8):
                block = zero
                for k in range(3):
                    block = jnp.where(index[k, 0, r] == b, pieces[k], block)
                edges[band, b * 128:(b + 1) * 128] = block
        loads[5].wait()
    with jax.named_scope("entry"):
        pl.semaphore_wait(barrier, VERT + TM - 2)

    def w1(i, q):
        return copy(weight.at[tile_rows, tile_cols[i]], wg.at[pos(4 * i), v, c],
                    w1_s.at[i], w1_r.at[i], {"vert": q})

    def w1_all(i):
        ref = wg.at[pos(4 * i), pl.ds(0, VERT - 1), c]
        return copy(ref, ref, w1_s.at[i], w1_r.at[i], {"vert": lax.rem(v + 1, VERT)})

    def wring(s, h, side):
        ref = wg.at[pos((1 - s, s - 1)[side]), pl.ds(16 * h, 16), c]
        return copy(ref, ref, wr_s.at[side, s, h], wr_r.at[side, s, h], to_tm(1 - 2 * side, c))

    def wring_in(s, h, side):
        ref = wg.at[pos((-s, s)[side]), pl.ds(16 * h, 16), c]
        return copy(ref, ref, wr_s.at[side, s, h], wr_r.at[side, s, h], to_tm(1 - 2 * side, c))

    def hpart(d, half):
        if half is None:
            return hwg.at[pos(d), c, x]
        return hwg.at[pos(d), c, x, :, pl.ds(half * 512, 512)]

    def up(part, sems, s):
        ref = part(1 - s, 0 if s == 4 else None)
        return copy(ref, ref, sems[0].at[s], sems[1].at[s], to_tm(1, c))

    def up_in(part, sems, s):
        ref = part(-s, 0 if s == 4 else None)
        return copy(ref, ref, sems[0].at[s], sems[1].at[s], to_tm(1, c))

    def down(part, sems, s):
        ref = part(s - 1, 1 if s == 4 else None)
        return copy(ref, ref, sems[0].at[s], sems[1].at[s], to_tm(-1, c))

    def down_in(part, sems, s):
        ref = part(s, 1 if s == 4 else None)
        return copy(ref, ref, sems[0].at[s], sems[1].at[s], to_tm(-1, c))

    hup, hdown = (hr_s, hr_r), (hl_s, hl_r)

    def ring_send(part, sems_up, sems_down, s):
        up(part, sems_up, s).start()
        down(part, sems_down, s).start()

    def ring_wait(part, sems_up, sems_down, s):
        up_in(part, sems_up, s).wait_recv()
        down_in(part, sems_down, s).wait_recv()

    def wpartner(d):
        ref = wg.at[pos(d), :, c]
        i = d % YS
        return copy(ref, ref, wp_s.at[i], wp_r.at[i], to_tm(0, 1 - c))

    def wpartner_in(d):
        ref = wg.at[pos(d), :, 1 - c]
        i = d % YS
        return copy(ref, ref, wp_s.at[i], wp_r.at[i], to_tm(0, 1 - c))

    def tiles(s):
        return (0,) if s == 0 else (4,) if s == 4 else (-s, s)

    def store(s, one, two):
        if s == 0:
            return one.at[0]
        if s == 4:
            return one.at[1]
        return two.at[s - 1]

    def width(s):
        return 128 * len(tiles(s))

    def boundary(s, q):
        return copy(store(s, picked_one, picked_two).at[q], store(s, recv_one, recv_two).at[v],
                    b_s.at[s], b_r.at[s], {"vert": q})

    def boundary_all(s):
        most = pl.ds(0, VERT - 1)
        return copy(store(s, picked_one, picked_two).at[most], store(s, recv_one, recv_two).at[most],
                    b_s.at[s], b_r.at[s], {"vert": lax.rem(v + 1, VERT)})

    def project(s):
        with jax.named_scope(f"project{s}"):
            parts = [wg[pos(d)].reshape(1024, 128) for d in tiles(s)]
            wide = parts[0] if len(parts) == 1 else jnp.concatenate(parts, axis=1)
            part = jnp.dot(feat[...], wide, preferred_element_type=F32).astype(BF16)
            store(s, proj_one, proj_two)[...] = part
            rows_out = jnp.dot(sel[...], part, preferred_element_type=F32).astype(BF16)
            picked = store(s, picked_one, picked_two)
            picked[...] = rows_out.reshape(VERT, 16, width(s))
            vert_peers(lambda q: boundary(s, q).start())
            store(s, recv_one, recv_two)[v] = picked[v]

    def regroup(ct, t):
        return copy(hid.at[ct, t], xg.at[ct, :, m], g_s.at[0], g_r.at[0], {"tm": t})

    def regroup_all():
        return copy(hid.at[:, pl.ds(0, TM - 1)], hid.at[:, pl.ds(0, TM - 1)],
                    g_s.at[0], g_r.at[0], to_tm(1, c))

    def convolve(s):
        with jax.named_scope(f"bwait{s}"):
            boundary_all(s).wait_recv()
        with jax.named_scope(f"convolve{s}"):
            part = store(s, proj_one, proj_two)[...]
            acc = part.astype(F32) + jnp.dot(edges[:, :512], part, preferred_element_type=F32)
            acc = acc + jnp.dot(
                edges[:, 512:], store(s, recv_one, recv_two)[...].reshape(512, width(s)),
                preferred_element_type=F32)
            done = jnp.maximum(acc, 0.0).astype(BF16)
            for i, d in enumerate(tiles(s)):
                hid[pos(d)] = done[:, i * 128:(i + 1) * 128].reshape(TM, 2, 16, 128)
            for d in tiles(s):
                tm_peers(lambda t: regroup(pos(d), t).start())
                xg[pos(d), :, m] = hid[pos(d), m]

    xr = lax.rem(x + 1, XS)
    xl = lax.rem(x + 3, XS)
    xo = lax.rem(x + 2, XS)
    sides = ({"vert": xr * 8 + z}, {"vert": xl * 8 + z})

    def x1(d, side):
        ref = hwg.at[pos(d), c, x]
        return copy(ref, ref, x1_s.at[side, d % YS], x1_r.at[side, d % YS], sides[side])

    def x1_in(d, side):
        ref = hwg.at[pos(d), c, (xl, xr)[side]]
        return copy(ref, ref, x1_s.at[side, d % YS], x1_r.at[side, d % YS], sides[side])

    def x2(d, side):
        ref = hwg.at[pos(d), c, (xl, xr)[side], :, pl.ds(512 * side, 512)]
        return copy(ref, ref, x2_s.at[side, d % YS], x2_r.at[side, d % YS], sides[side])

    def x2_in(d, side):
        ref = hwg.at[pos(d), c, xo, :, pl.ds(512 * side, 512)]
        return copy(ref, ref, x2_s.at[side, d % YS], x2_r.at[side, d % YS], sides[side])

    def hpartner(d):
        ref = hwg.at[pos(d), c]
        return copy(ref, ref, hp_s.at[d % YS], hp_r.at[d % YS], to_tm(0, 1 - c))

    def hpartner_in(d):
        ref = hwg.at[pos(d), 1 - c]
        return copy(ref, ref, hp_s.at[d % YS], hp_r.at[d % YS], to_tm(0, 1 - c))

    def x1_send(s):
        for d in tiles(s):
            for side in range(2):
                x1(d, side).start()

    def x2_send(s):
        with jax.named_scope(f"xwait{s}"):
            for d in tiles(s):
                for side in range(2):
                    x1_in(d, side).wait_recv()
                for side in range(2):
                    x2(d, side).start()

    def xdone(s):
        with jax.named_scope(f"xdone{s}"):
            for d in tiles(s):
                for side in range(2):
                    x2_in(d, side).wait_recv()
                hpartner(d).start()

    def wstep(s):
        with jax.named_scope(f"wstep{s}"):
            for h in range(2):
                for side in range(2):
                    wring_in(s, h, side).wait_recv()
                if s < 3:
                    for side in range(2):
                        wring(s + 1, h, side).start()
            for d in tiles(s):
                wpartner(d).start()

    def hstep(s):
        with jax.named_scope(f"hstep{s}"):
            ring_wait(hpart, hup, hdown, s)
            if s < 4:
                ring_send(hpart, hup, hdown, s + 1)

    def wready(s):
        with jax.named_scope(f"wready{s}"):
            for d in tiles(s):
                wpartner_in(d).wait_recv()

    def w1_wait(i):
        with jax.named_scope(f"wtiles{i}"):
            w1_all(i).wait_recv()
            wpartner(4 * i).start()

    vert_peers(lambda q: w1(0, q).start())
    ring_send(hpart, hup, hdown, 1)
    x1_send(0)
    vert_peers(lambda q: w1(1, q).start())
    hstep(1)
    x1_send(1)
    w1_wait(0)
    for h in range(2):
        for side in range(2):
            wring(1, h, side).start()
    loads[6].wait()
    wready(0)
    project(0)
    w1_wait(1)
    wstep(1)
    hstep(2)
    wready(1)
    project(1)
    x1_send(2)
    x2_send(0)
    wstep(2)
    convolve(0)
    wready(2)
    project(2)
    hstep(3)
    x1_send(3)
    wstep(3)
    convolve(1)
    wready(3)
    project(3)
    wready(4)
    project(4)
    x2_send(1)
    convolve(2)
    hstep(4)
    x1_send(4)
    xdone(0)
    convolve(3)
    convolve(4)
    x2_send(2)
    xdone(1)
    with jax.named_scope("gwait"):
        regroup_all().wait_recv()

    order = (0, 1, -1, 2, -2, 3, -3, 4)

    def give(i, t):
        return copy(att.at[i, :, t], ret.at[i, m], a_s.at[0], a_r.at[i], {"tm": t})

    def give_all(i):
        most = pl.ds(0, TM - 1)
        return copy(ret.at[i, most], ret.at[i, most], a_s.at[0], a_r.at[i], to_tm(1, c))

    def give_out():
        most = pl.ds(0, TM - 1)
        return copy(ret.at[:, most], ret.at[:, most], a_s.at[0], a_r.at[0], to_tm(1, c))

    def attend(i):
        with jax.named_scope(f"hready{i}"):
            hpartner_in(order[i]).wait_recv()
        with jax.named_scope(f"attend{i}"):
            wide = hwg[pos(order[i])].reshape(384, 1024)
            packed = None
            for ch in range(4):
                seen = jnp.concatenate(
                    [xg[2 * ch].reshape(512, 128), xg[2 * ch + 1].reshape(512, 128)], axis=1)
                term = dot_last(wide[:, ch * WIDE:(ch + 1) * WIDE], seen)
                packed = term if packed is None else packed + term
            packed = packed.astype(BF16)
            for b in range(2):
                cols = slice(b * 256, (b + 1) * 256)
                outs = []
                for j in range(2):
                    query = packed[192 * j:192 * j + 64, cols]
                    key = packed[192 * j + 64:192 * j + 128, cols]
                    value = packed[192 * j + 128:192 * j + 192, cols]
                    score = dot_first(key, query) * 0.125 + bias[...]
                    top = jnp.max(score, axis=0, keepdims=True)
                    exponent = jnp.exp(score - top)
                    scale = 1.0 / jnp.sum(exponent, axis=0, keepdims=True)
                    attention = (exponent * scale).astype(BF16)
                    outs.append(jnp.dot(value, attention, preferred_element_type=F32))
                block = jnp.concatenate(outs, axis=0)
                att[i, b] = block.T.astype(BF16).reshape(TM, 16, 128)
            tm_peers(lambda t: give(i, t).start())
            ret[i, m] = att[i, :, m]

    for i in range(YS):
        attend(i)
        if i == 0:
            x2_send(3)
            xdone(2)
        if i == 1:
            x2_send(4)
        if i == 3:
            xdone(3)
        if i == 5:
            xdone(4)

    with jax.named_scope("sent"):
        for i in range(2):
            w1_all(i).wait_send()
        for s in range(1, 5):
            if s < 4:
                for h in range(2):
                    for side in range(2):
                        wring(s, h, side).wait_send()
            up(hpart, hup, s).wait_send()
            down(hpart, hdown, s).wait_send()
        for d in range(YS):
            wpartner(d).wait_send()
            for side in range(2):
                x1(d, side).wait_send()
                x2(d, side).wait_send()
            hpartner(d).wait_send()
        for s in range(STEPS):
            boundary_all(s).wait_send()
        regroup_all().wait_send()

    for i in range(YS):
        with jax.named_scope(f"await{i}"):
            give_all(i).wait_recv()
        for yy in range(YS):
            ct = (yy + order[i]) % YS
            pair = pl.ds(2 * yy, 2)
            total = (hid[ct, pair].reshape(64, 128).astype(F32)
                     + ret[i, pair].reshape(64, 128).astype(F32))
            out[yy * 64:(yy + 1) * 64, ct * 128:(ct + 1) * 128] = total.astype(BF16)
    with jax.named_scope("last"):
        give_out().wait_send()


def layer(*operands):
    dma = pltpu.SemaphoreType.DMA
    vmem = pl.BlockSpec(memory_space=pltpu.VMEM)
    hbm = pl.BlockSpec(memory_space=pltpu.HBM)
    return pl.pallas_call(
        layer_kernel,
        out_shape=jax.ShapeDtypeStruct((512, 1024), BF16),
        in_specs=[hbm] * 7,
        out_specs=vmem,
        scratch_shapes=[
            pltpu.VMEM((512, 1024), BF16),
            pltpu.VMEM((32, 1024), BF16),
            pltpu.VMEM((16, VERT), jnp.int32),
            pltpu.VMEM((1, VERT), jnp.int32),
            pltpu.VMEM((3, 512, 128), BF16),
            pltpu.SMEM((3, 1, 4), jnp.int32),
            pltpu.VMEM((YS, VERT, 2, 16, 128), BF16),
            pltpu.VMEM((YS, 2, XS, 48, 1024), BF16),
            pltpu.VMEM((2, 512, 128), BF16),
            pltpu.VMEM((3, 512, WIDE), BF16),
            pltpu.VMEM((2, VERT, 16, 128), BF16),
            pltpu.VMEM((3, VERT, 16, WIDE), BF16),
            pltpu.VMEM((2, VERT, 16, 128), BF16),
            pltpu.VMEM((3, VERT, 16, WIDE), BF16),
            pltpu.VMEM((YS, TM, 2, 16, 128), BF16),
            pltpu.VMEM((YS, 2, TM, 16, 128), BF16),
            pltpu.VMEM((YS, 2, TM, 16, 128), BF16),
            pltpu.VMEM((YS, TM, 2, 16, 128), BF16),
            pltpu.VMEM((512, 512), BF16),
            pltpu.VMEM((512, 1024), BF16),
            pltpu.VMEM((256, 256), F32),
            dma((7,)), dma((2,)), dma((2,)),
            dma((2, 4, 2)), dma((2, 4, 2)), dma((YS,)), dma((YS,)),
            dma((5,)), dma((5,)), dma((5,)), dma((5,)),
            dma((2, YS)), dma((2, YS)), dma((2, YS)), dma((2, YS)),
            dma((YS,)), dma((YS,)),
            dma((STEPS,)), dma((STEPS,)),
            dma((1,)), dma((1,)),
            dma((1,)), dma((YS,)),
        ],
        compiler_params=pltpu.CompilerParams(
            collective_id=0, has_side_effects=True, vmem_limit_bytes=48 * 1024 * 1024),
    )(*(pltpu.with_memory_space_constraint(op, pltpu.HBM) for op in operands))


def shards(features, graph_weight, head_weight, send_rows, send_count, block_index, block_values):
    heads = head_weight[0].reshape(XS, 48, 1024)
    return layer(
        features[0], graph_weight, heads, send_rows[0, 0].T, send_count[0],
        block_values[0].transpose(1, 0, 2), block_index.transpose(2, 0, 1))[None]


def solution(mesh):
    return jax.shard_map(
        shards,
        mesh=mesh,
        in_specs=(
            P("tm", "vert", None),
            P("vert", None),
            P("tm", None, None),
            P("tm", "vert", None, None),
            P("tm", "vert", None),
            P("tm", "vert", None),
            P("tm", "vert", None, None),
        ),
        out_specs=P("tm", "vert", None),
        check_vma=False,
    )
```

```python
import jax
import jax.numpy as jnp
from jax import lax
from jax.experimental import pallas as pl
from jax.experimental.pallas import tpu as pltpu
from jax.sharding import PartitionSpec as P

BF16 = jnp.bfloat16
F32 = jnp.float32
VERT = 32
TM = 16
YS = 8
XS = 4
WIDE = 256
STEPS = 5
MESH = pl.DeviceIdType.MESH


def dot_last(left, right):
    return lax.dot_general(left, right, (((1,), (1,)), ((), ())), preferred_element_type=F32)


def dot_first(left, right):
    return lax.dot_general(left, right, (((0,), (0,)), ((), ())), preferred_element_type=F32)


def layer_kernel(
    feat_in, weight_in, heads, rows_in, count_in, blocks_in, index_in, out,
    feat, weight, rows, count, blocks, index,
    wg, hwg, proj_one, proj_two, picked_one, picked_two, recv_one, recv_two,
    hid, xg, att, ret, sel, edges, bias,
    in_s, w1_s, w1_r, wr_s, wr_r, wp_s, wp_r,
    hr_s, hr_r, hl_s, hl_r, x1_s, x1_r, x2_s, x2_r, hp_s, hp_r,
    b_s, b_r, g_s, g_r, a_s, a_r,
):
    v = lax.axis_index("vert")
    m = lax.axis_index("tm")
    y = m // 2
    c = lax.rem(m, 2)
    x = v // 8
    z = lax.rem(v, 8)

    def pos(d):
        return lax.rem(y + d + 2 * YS, YS)

    def to_tm(d, cc):
        return {"tm": pos(d) * 2 + cc}

    def copy(src, dst, ssem, rsem, dev):
        return pltpu.make_async_remote_copy(
            src_ref=src, dst_ref=dst, send_sem=ssem, recv_sem=rsem,
            device_id=dev, device_id_type=MESH,
        )

    def loop(lo, hi, body):
        def step(i, carry):
            body(i)
            return carry
        lax.fori_loop(lo, hi, step, 0)

    by_x = [lax.rem(x + dx, XS) * 8 for dx in range(XS)]
    by_z = [lax.rem(z + dz, 8) for dz in range(8)]
    vert_ids = [by_x[dx] + by_z[dz] for dx in (2, 1, 3, 0) for dz in (4, 3, 5, 2, 6, 1, 7, 0)][:-1]
    by_y = [lax.rem(y + dy, YS) * 2 for dy in range(YS)]
    tm_ids = [by_y[dy] + cc for dy in (4, 3, 5, 2, 6, 1, 7, 0) for cc in (1 - c, c)][:-1]

    def vert_peers(body):
        for q in vert_ids:
            body(q)

    def tm_peers(body):
        for t in tm_ids:
            body(t)

    barrier = pltpu.get_barrier_semaphore()
    vert_peers(lambda q: pl.semaphore_signal(barrier, inc=1, device_id={"vert": q}, device_id_type=MESH))
    tm_peers(lambda t: pl.semaphore_signal(barrier, inc=1, device_id={"tm": t}, device_id_type=MESH))

    loads = [
        pltpu.make_async_copy(src, dst, in_s.at[i]) for i, (src, dst) in enumerate((
            (rows_in, rows), (count_in, count), (index_in, index), (blocks_in, blocks),
            (weight_in, weight), (heads.at[x], hwg.at[y, c, x]), (feat_in, feat)))
    ]
    for load in loads:
        load.start()

    tile_cols = [pl.ds(pl.multiple_of(pos(4 * i) * 128, 128), 128) for i in range(2)]
    tile_rows = pl.ds(pl.multiple_of(c * 16, 16), 16)

    with jax.named_scope("tables"):
        ri = lax.broadcasted_iota(jnp.int32, (256, 256), 0)
        ci = lax.broadcasted_iota(jnp.int32, (256, 256), 1)
        bias[...] = jnp.where(((ri & 15) == (ci & 15)) & (ri <= ci), 0.0, -1e30)
        for load in loads[:5]:
            load.wait()
        for i in range(2):
            wg[pos(4 * i), v, c] = weight[tile_rows, tile_cols[i]]
        live = lax.broadcasted_iota(jnp.int32, (16, VERT), 0) < count[...]
        slots = jnp.where(live, rows[...], 1023)
        lane = lax.broadcasted_iota(jnp.int32, (VERT, 512), 1)
        spread = (lane // 16 == lax.broadcasted_iota(jnp.int32, (VERT, 512), 0)).astype(BF16)
        high = jnp.dot((slots >> 4).astype(F32).astype(BF16), spread, preferred_element_type=F32)
        low = jnp.dot((slots & 15).astype(F32).astype(BF16), spread, preferred_element_type=F32)
        slot = lax.broadcasted_iota(jnp.int32, (16, 512), 0)
        mine = slot == (lax.broadcasted_iota(jnp.int32, (16, 512), 1) & 15)
        wanted = jnp.sum(jnp.where(mine, high * 16.0 + low, 0.0), axis=0, keepdims=True)
        vertex = lax.broadcasted_iota(jnp.int32, (512, 512), 0).astype(F32)
        sel[...] = jnp.where(vertex == wanted, 1.0, 0.0).T.astype(BF16)
        for r in range(4):
            band = slice(r * 128, (r + 1) * 128)
            pieces = [blocks[k, band] for k in range(3)]
            zero = jnp.zeros((128, 128), BF16)
            for b in range(8):
                block = zero
                for k in range(3):
                    block = jnp.where(index[k, 0, r] == b, pieces[k], block)
                edges[band, b * 128:(b + 1) * 128] = block
        loads[5].wait()
    with jax.named_scope("entry"):
        pl.semaphore_wait(barrier, VERT + TM - 2)

    def w1(i, q):
        return copy(weight.at[tile_rows, tile_cols[i]], wg.at[pos(4 * i), v, c],
                    w1_s.at[i], w1_r.at[i], {"vert": q})

    def w1_all(i):
        ref = wg.at[pos(4 * i), pl.ds(0, VERT - 1), c]
        return copy(ref, ref, w1_s.at[i], w1_r.at[i], {"vert": lax.rem(v + 1, VERT)})

    def wring(s, h, side):
        ref = wg.at[pos((1 - s, s - 1)[side]), pl.ds(16 * h, 16), c]
        return copy(ref, ref, wr_s.at[side, s, h], wr_r.at[side, s, h], to_tm(1 - 2 * side, c))

    def wring_in(s, h, side):
        ref = wg.at[pos((-s, s)[side]), pl.ds(16 * h, 16), c]
        return copy(ref, ref, wr_s.at[side, s, h], wr_r.at[side, s, h], to_tm(1 - 2 * side, c))

    def hpart(d, half):
        if half is None:
            return hwg.at[pos(d), c, x]
        return hwg.at[pos(d), c, x, :, pl.ds(half * 512, 512)]

    def up(part, sems, s):
        ref = part(1 - s, 0 if s == 4 else None)
        return copy(ref, ref, sems[0].at[s], sems[1].at[s], to_tm(1, c))

    def up_in(part, sems, s):
        ref = part(-s, 0 if s == 4 else None)
        return copy(ref, ref, sems[0].at[s], sems[1].at[s], to_tm(1, c))

    def down(part, sems, s):
        ref = part(s - 1, 1 if s == 4 else None)
        return copy(ref, ref, sems[0].at[s], sems[1].at[s], to_tm(-1, c))

    def down_in(part, sems, s):
        ref = part(s, 1 if s == 4 else None)
        return copy(ref, ref, sems[0].at[s], sems[1].at[s], to_tm(-1, c))

    hup, hdown = (hr_s, hr_r), (hl_s, hl_r)

    def ring_send(part, sems_up, sems_down, s):
        up(part, sems_up, s).start()
        down(part, sems_down, s).start()

    def ring_wait(part, sems_up, sems_down, s):
        up_in(part, sems_up, s).wait_recv()
        down_in(part, sems_down, s).wait_recv()

    def wpartner(d):
        ref = wg.at[pos(d), :, c]
        i = d % YS
        return copy(ref, ref, wp_s.at[i], wp_r.at[i], to_tm(0, 1 - c))

    def wpartner_in(d):
        ref = wg.at[pos(d), :, 1 - c]
        i = d % YS
        return copy(ref, ref, wp_s.at[i], wp_r.at[i], to_tm(0, 1 - c))

    def tiles(s):
        return (0,) if s == 0 else (4,) if s == 4 else (-s, s)

    def store(s, one, two):
        if s == 0:
            return one.at[0]
        if s == 4:
            return one.at[1]
        return two.at[s - 1]

    def width(s):
        return 128 * len(tiles(s))

    def boundary(s, q):
        return copy(store(s, picked_one, picked_two).at[q], store(s, recv_one, recv_two).at[v],
                    b_s.at[s], b_r.at[s], {"vert": q})

    def boundary_all(s):
        most = pl.ds(0, VERT - 1)
        return copy(store(s, picked_one, picked_two).at[most], store(s, recv_one, recv_two).at[most],
                    b_s.at[s], b_r.at[s], {"vert": lax.rem(v + 1, VERT)})

    def project(s):
        with jax.named_scope(f"project{s}"):
            parts = [wg[pos(d)].reshape(1024, 128) for d in tiles(s)]
            wide = parts[0] if len(parts) == 1 else jnp.concatenate(parts, axis=1)
            part = jnp.dot(feat[...], wide, preferred_element_type=F32).astype(BF16)
            store(s, proj_one, proj_two)[...] = part
            rows_out = jnp.dot(sel[...], part, preferred_element_type=F32).astype(BF16)
            picked = store(s, picked_one, picked_two)
            picked[...] = rows_out.reshape(VERT, 16, width(s))
            vert_peers(lambda q: boundary(s, q).start())
            store(s, recv_one, recv_two)[v] = picked[v]

    def regroup(ct, t):
        return copy(hid.at[ct, t], xg.at[ct, :, m], g_s.at[0], g_r.at[0], {"tm": t})

    def regroup_all():
        return copy(hid.at[:, pl.ds(0, TM - 1)], hid.at[:, pl.ds(0, TM - 1)],
                    g_s.at[0], g_r.at[0], to_tm(1, c))

    def convolve(s):
        with jax.named_scope(f"bwait{s}"):
            boundary_all(s).wait_recv()
        with jax.named_scope(f"convolve{s}"):
            part = store(s, proj_one, proj_two)[...]
            acc = part.astype(F32) + jnp.dot(edges[:, :512], part, preferred_element_type=F32)
            acc = acc + jnp.dot(
                edges[:, 512:], store(s, recv_one, recv_two)[...].reshape(512, width(s)),
                preferred_element_type=F32)
            done = jnp.maximum(acc, 0.0).astype(BF16)
            for i, d in enumerate(tiles(s)):
                hid[pos(d)] = done[:, i * 128:(i + 1) * 128].reshape(TM, 2, 16, 128)
            for d in tiles(s):
                tm_peers(lambda t: regroup(pos(d), t).start())
                xg[pos(d), :, m] = hid[pos(d), m]

    xr = lax.rem(x + 1, XS)
    xl = lax.rem(x + 3, XS)
    xo = lax.rem(x + 2, XS)
    sides = ({"vert": xr * 8 + z}, {"vert": xl * 8 + z})

    def x1(d, side):
        ref = hwg.at[pos(d), c, x]
        return copy(ref, ref, x1_s.at[side, d % YS], x1_r.at[side, d % YS], sides[side])

    def x1_in(d, side):
        ref = hwg.at[pos(d), c, (xl, xr)[side]]
        return copy(ref, ref, x1_s.at[side, d % YS], x1_r.at[side, d % YS], sides[side])

    def x2(d, side):
        ref = hwg.at[pos(d), c, (xl, xr)[side], :, pl.ds(512 * side, 512)]
        return copy(ref, ref, x2_s.at[side, d % YS], x2_r.at[side, d % YS], sides[side])

    def x2_in(d, side):
        ref = hwg.at[pos(d), c, xo, :, pl.ds(512 * side, 512)]
        return copy(ref, ref, x2_s.at[side, d % YS], x2_r.at[side, d % YS], sides[side])

    def hpartner(d):
        ref = hwg.at[pos(d), c]
        return copy(ref, ref, hp_s.at[d % YS], hp_r.at[d % YS], to_tm(0, 1 - c))

    def hpartner_in(d):
        ref = hwg.at[pos(d), 1 - c]
        return copy(ref, ref, hp_s.at[d % YS], hp_r.at[d % YS], to_tm(0, 1 - c))

    def x1_send(s):
        for d in tiles(s):
            for side in range(2):
                x1(d, side).start()

    def x2_send(s):
        with jax.named_scope(f"xwait{s}"):
            for d in tiles(s):
                for side in range(2):
                    x1_in(d, side).wait_recv()
                for side in range(2):
                    x2(d, side).start()

    def xdone(s):
        with jax.named_scope(f"xdone{s}"):
            for d in tiles(s):
                for side in range(2):
                    x2_in(d, side).wait_recv()
                hpartner(d).start()

    def wstep(s):
        with jax.named_scope(f"wstep{s}"):
            for h in range(2):
                for side in range(2):
                    wring_in(s, h, side).wait_recv()
                if s < 3:
                    for side in range(2):
                        wring(s + 1, h, side).start()
            for d in tiles(s):
                wpartner(d).start()

    def hstep(s):
        with jax.named_scope(f"hstep{s}"):
            ring_wait(hpart, hup, hdown, s)
            if s < 4:
                ring_send(hpart, hup, hdown, s + 1)

    def wready(s):
        with jax.named_scope(f"wready{s}"):
            for d in tiles(s):
                wpartner_in(d).wait_recv()

    def w1_wait(i):
        with jax.named_scope(f"wtiles{i}"):
            w1_all(i).wait_recv()
            wpartner(4 * i).start()

    vert_peers(lambda q: w1(0, q).start())
    ring_send(hpart, hup, hdown, 1)
    hstep(1)
    vert_peers(lambda q: w1(1, q).start())
    x1_send(0)
    x1_send(1)
    w1_wait(0)
    for h in range(2):
        for side in range(2):
            wring(1, h, side).start()
    loads[6].wait()
    wready(0)
    project(0)
    wstep(1)
    hstep(2)
    wready(1)
    project(1)
    w1_wait(1)
    x1_send(2)
    x2_send(0)
    wstep(2)
    convolve(0)
    wready(2)
    project(2)
    hstep(3)
    x1_send(3)
    wstep(3)
    convolve(1)
    wready(3)
    project(3)
    wready(4)
    project(4)
    x2_send(1)
    convolve(2)
    hstep(4)
    x1_send(4)
    xdone(0)
    convolve(3)
    convolve(4)
    x2_send(2)
    xdone(1)
    with jax.named_scope("gwait"):
        regroup_all().wait_recv()

    order = (0, 1, -1, 2, -2, 3, -3, 4)

    def give(i, t):
        return copy(att.at[i, :, t], ret.at[i, m], a_s.at[0], a_r.at[i], {"tm": t})

    def give_half(b, t):
        return copy(att.at[0, b, t], ret.at[0, m, b], a_s.at[0], a_r.at[0], {"tm": t})

    def give_all(i):
        most = pl.ds(0, TM - 1)
        return copy(ret.at[i, most], ret.at[i, most], a_s.at[0], a_r.at[i], to_tm(1, c))

    def give_out():
        most = pl.ds(0, TM - 1)
        return copy(ret.at[:, most], ret.at[:, most], a_s.at[0], a_r.at[0], to_tm(1, c))

    def attend(i):
        with jax.named_scope(f"hready{i}"):
            hpartner_in(order[i]).wait_recv()
        with jax.named_scope(f"attend{i}"):
            wide = hwg[pos(order[i])].reshape(384, 1024)
            for part in ((0,), (1,)) if i == 0 else ((0, 1),):
                count_rows = 256 * len(part)
                packed = None
                for ch in range(4):
                    seen = jnp.concatenate(
                        [xg[ct, part[0]:part[-1] + 1].reshape(count_rows, 128)
                         for ct in (2 * ch, 2 * ch + 1)], axis=1)
                    term = dot_last(wide[:, ch * WIDE:(ch + 1) * WIDE], seen)
                    packed = term if packed is None else packed + term
                packed = packed.astype(BF16)
                for n, b in enumerate(part):
                    cols = slice(n * 256, (n + 1) * 256)
                    outs = []
                    for j in range(2):
                        query = packed[192 * j:192 * j + 64, cols]
                        key = packed[192 * j + 64:192 * j + 128, cols]
                        value = packed[192 * j + 128:192 * j + 192, cols]
                        score = dot_first(key, query) * 0.125 + bias[...]
                        top = jnp.max(score, axis=0, keepdims=True)
                        exponent = jnp.exp(score - top)
                        scale = 1.0 / jnp.sum(exponent, axis=0, keepdims=True)
                        attention = (exponent * scale).astype(BF16)
                        outs.append(jnp.dot(value, attention, preferred_element_type=F32))
                    block = jnp.concatenate(outs, axis=0)
                    att[i, b] = block.T.astype(BF16).reshape(TM, 16, 128)
                    if i == 0:
                        tm_peers(lambda t: give_half(b, t).start())
            if i > 0:
                tm_peers(lambda t: give(i, t).start())
            ret[i, m] = att[i, :, m]

    for i in range(YS):
        attend(i)
        if i == 0:
            x2_send(3)
            xdone(2)
        if i == 1:
            x2_send(4)
        if i == 3:
            xdone(3)
        if i == 5:
            xdone(4)

    with jax.named_scope("sent"):
        for i in range(2):
            w1_all(i).wait_send()
        for s in range(1, 5):
            if s < 4:
                for h in range(2):
                    for side in range(2):
                        wring(s, h, side).wait_send()
            up(hpart, hup, s).wait_send()
            down(hpart, hdown, s).wait_send()
        for d in range(YS):
            wpartner(d).wait_send()
            for side in range(2):
                x1(d, side).wait_send()
                x2(d, side).wait_send()
            hpartner(d).wait_send()
        for s in range(STEPS):
            boundary_all(s).wait_send()
        regroup_all().wait_send()

    for i in range(YS):
        with jax.named_scope(f"await{i}"):
            give_all(i).wait_recv()
        for yy in range(YS):
            ct = (yy + order[i]) % YS
            pair = pl.ds(2 * yy, 2)
            total = (hid[ct, pair].reshape(64, 128).astype(F32)
                     + ret[i, pair].reshape(64, 128).astype(F32))
            out[yy * 64:(yy + 1) * 64, ct * 128:(ct + 1) * 128] = total.astype(BF16)
    with jax.named_scope("last"):
        give_out().wait_send()


def layer(*operands):
    dma = pltpu.SemaphoreType.DMA
    vmem = pl.BlockSpec(memory_space=pltpu.VMEM)
    hbm = pl.BlockSpec(memory_space=pltpu.HBM)
    return pl.pallas_call(
        layer_kernel,
        out_shape=jax.ShapeDtypeStruct((512, 1024), BF16),
        in_specs=[hbm] * 7,
        out_specs=vmem,
        scratch_shapes=[
            pltpu.VMEM((512, 1024), BF16),
            pltpu.VMEM((32, 1024), BF16),
            pltpu.VMEM((16, VERT), jnp.int32),
            pltpu.VMEM((1, VERT), jnp.int32),
            pltpu.VMEM((3, 512, 128), BF16),
            pltpu.SMEM((3, 1, 4), jnp.int32),
            pltpu.VMEM((YS, VERT, 2, 16, 128), BF16),
            pltpu.VMEM((YS, 2, XS, 48, 1024), BF16),
            pltpu.VMEM((2, 512, 128), BF16),
            pltpu.VMEM((3, 512, WIDE), BF16),
            pltpu.VMEM((2, VERT, 16, 128), BF16),
            pltpu.VMEM((3, VERT, 16, WIDE), BF16),
            pltpu.VMEM((2, VERT, 16, 128), BF16),
            pltpu.VMEM((3, VERT, 16, WIDE), BF16),
            pltpu.VMEM((YS, TM, 2, 16, 128), BF16),
            pltpu.VMEM((YS, 2, TM, 16, 128), BF16),
            pltpu.VMEM((YS, 2, TM, 16, 128), BF16),
            pltpu.VMEM((YS, TM, 2, 16, 128), BF16),
            pltpu.VMEM((512, 512), BF16),
            pltpu.VMEM((512, 1024), BF16),
            pltpu.VMEM((256, 256), F32),
            dma((7,)), dma((2,)), dma((2,)),
            dma((2, 4, 2)), dma((2, 4, 2)), dma((YS,)), dma((YS,)),
            dma((5,)), dma((5,)), dma((5,)), dma((5,)),
            dma((2, YS)), dma((2, YS)), dma((2, YS)), dma((2, YS)),
            dma((YS,)), dma((YS,)),
            dma((STEPS,)), dma((STEPS,)),
            dma((1,)), dma((1,)),
            dma((1,)), dma((YS,)),
        ],
        compiler_params=pltpu.CompilerParams(
            collective_id=0, has_side_effects=True, vmem_limit_bytes=48 * 1024 * 1024),
    )(*(pltpu.with_memory_space_constraint(op, pltpu.HBM) for op in operands))


def shards(features, graph_weight, head_weight, send_rows, send_count, block_index, block_values):
    heads = head_weight[0].reshape(XS, 48, 1024)
    return layer(
        features[0], graph_weight, heads, send_rows[0, 0].T, send_count[0],
        block_values[0].transpose(1, 0, 2), block_index.transpose(2, 0, 1))[None]


def solution(mesh):
    return jax.shard_map(
        shards,
        mesh=mesh,
        in_specs=(
            P("tm", "vert", None),
            P("vert", None),
            P("tm", None, None),
            P("tm", "vert", None, None),
            P("tm", "vert", None),
            P("tm", "vert", None),
            P("tm", "vert", None, None),
        ),
        out_specs=P("tm", "vert", None),
        check_vma=False,
    )
```
